32 devices in a mesh: mem: 8 (over y, x, core), reg: 4 (over z).
Axes of the slice: x: 2, y: 2, z: 4, core: 2. Of those that a mesh axis runs over, the one named last changes fastest.
Arguments:
- sample_stack: float32 [64, 11, 8, 256], P('mem', None, 'reg'), may hold values from -6 to 6
- weights: float32 [4, 64], P('reg', 'mem'), may hold values from 0.1 to 10
- offspring: int32 [4, 64], P('reg'), may hold values from 0 to 63
- localize: float32 [8, 256], P('reg'), may hold values from 0.2 to 0.9
Outputs:
- posterior: float32 [64, 11, 8, 256], P('mem', None, 'reg')
The draws below stay inside these ranges and needn't reach their ends.
Inputs may be any that keep to these rules, and one draw needn't show every extreme that they name: `offspring`: each entry names a member.
All inputs are finite; a program needn't handle non-finite values.
Results may differ from the reference program's by a relative error of at most 0.0021.
Values may be sent and summed in bfloat16 or wider, within the bound.
A program may use at most 64 MiB of HBM per device.

```python
import math
import jax
import jax.numpy as jnp
import numpy as np
from jax import lax

VERTICAL_QUANTS = 11
BAND_LATITUDES = 2
LATTICE_WIDTH = 256
SAMPLE_TOTAL = 64
ZONE_BANDS_NUM = 4
NY = 8


def with_ends(values, rng, least, high):
    spot = [jax.random.randint(jax.random.fold_in(rng, axis), (), 0, length) for axis, length in enumerate(values.shape)]
    longest = values.shape.index(max(values.shape))
    next_to = spot[:longest] + [(spot[longest] + 1) % values.shape[longest]] + spot[longest + 1:]
    return values.at[tuple(spot)].set(least).at[tuple(next_to)].set(high)


def block_scale(stream_key, dims, split, smallest, largest):
    def one(dim, shards_of):
        steps = jax.random.uniform(jax.random.fold_in(jax.random.fold_in(stream_key, 6), dim), (shards_of,), jnp.float32, smallest / len(split), largest / len(split))
        return jnp.repeat(jnp.exp(steps), dims[dim] // shards_of).reshape((-1,) + (1,) * (len(dims) - dim - 1))

    factor_of = one(*split[0])
    for cut in split[1:]:
        factor_of = factor_of * one(*cut)
    return factor_of


def cumulative_ranks(count, slope):
    portions = [(1 << 20) // math.isqrt(grade ** slope) + 1 for grade in range(1, count + 1)]
    width = 1 + sum(portions) // (1 << 30)
    return np.cumsum(np.array([max(1, weight // width) for weight in portions]))


def skewed_ids(stream_key, shape, number_of, skew):
    table = cumulative_ranks(number_of, skew)
    pick = jax.random.randint(jax.random.fold_in(stream_key, 1), shape, 0, int(table[number_of - 1]))
    standing = jnp.searchsorted(jnp.asarray(table, jnp.int32), pick, side="right")
    return jax.random.permutation(jax.random.fold_in(stream_key, 2), number_of)[standing].astype(jnp.int32)


def noise(stream_key, dims, scale, reach, pieces=(), dtype=jnp.bfloat16):
    values = jax.random.normal(stream_key, dims, jnp.float32) * scale
    if len(pieces) > 0:
        values = block_scale(stream_key, dims, pieces, -0.22, 0.18) * values
    return jnp.clip(values, min=-reach, max=reach).astype(dtype)


def setup_inputs(seed: int = 0) -> dict:
    key_list = jax.random.split(jax.random.key(seed), 5)
    return {
        "sample_stack": noise(key_list[0], (SAMPLE_TOTAL, VERTICAL_QUANTS, NY, LATTICE_WIDTH), 1.0, 6.0, ((0, 8), (2, 4)), jnp.float32),
        "weights": jnp.clip(jnp.exp(math.log(10.0) - 4.6051702 * jax.random.uniform(key_list[1], (ZONE_BANDS_NUM, SAMPLE_TOTAL), jnp.float32) ** block_scale(key_list[1], (ZONE_BANDS_NUM, SAMPLE_TOTAL), ((0, 4), (1, 8)), -0.2, 0.2)), 0.1, 10.0),
        "offspring": with_ends(skewed_ids(key_list[2], (ZONE_BANDS_NUM, SAMPLE_TOTAL), SAMPLE_TOTAL, 2), jax.random.fold_in(key_list[2], 3), 0, SAMPLE_TOTAL - 1).astype(jnp.int32),
        "localize": jnp.clip(0.2 + 0.7 * jax.random.uniform(key_list[3], (NY, LATTICE_WIDTH), jnp.float32) ** block_scale(key_list[3], (NY, LATTICE_WIDTH), ((0, 4),), -0.2, 0.2), 0.2, 0.9),
    }


wave_gain = 0.25
advect_gain = 0.1
diffuse_gain = 0.1
small_eps = 1e-05

def advance(padded):
    centre = padded[:, :, 1:-1]
    upper_rows = padded[:, :, 2:]
    lower_rows = padded[:, :, :-2]
    right_cols = jnp.roll(centre, -1, 3)
    left_cols = jnp.roll(centre, 1, 3)
    slope_east = 0.5 * (right_cols - left_cols)
    slope_north = 0.5 * (upper_rows - lower_rows)
    laplace = right_cols + left_cols + upper_rows + lower_rows - 4.0 * centre
    height = centre[:, 0]
    flow_east = centre[:, 1]
    flow_north = centre[:, 2]
    tracer = centre[:, 3:]
    new_height = height - wave_gain * (slope_east[:, 1] + slope_north[:, 2])
    new_east = flow_east - wave_gain * slope_east[:, 0]
    new_north = flow_north - wave_gain * slope_north[:, 0]
    new_tracer = tracer - advect_gain * (flow_east[:, None] * slope_east[:, 3:] + flow_north[:, None] * slope_north[:, 3:]) + diffuse_gain * laplace[:, 3:]
    return jnp.concatenate([new_height[:, None], new_east[:, None], new_north[:, None], new_tracer], axis=1)

def propagate_dynamics(model_snapshot):
    padded = jnp.concatenate([model_snapshot[:, :, -1:], model_snapshot, model_snapshot[:, :, :1]], axis=2)
    return advance(padded)

def reference(sample_stack, weights, offspring, localize):
    background_prediction = propagate_dynamics(propagate_dynamics(sample_stack))
    band_partition = background_prediction.reshape(SAMPLE_TOTAL, VERTICAL_QUANTS, ZONE_BANDS_NUM, BAND_LATITUDES, LATTICE_WIDTH)
    importance_factors = jnp.transpose(weights)[:, None, :, None, None]
    weight_total = lax.optimization_barrier(jnp.sum(weights, axis=1))[None, :, None, None]
    sample_average_map = lax.optimization_barrier(jnp.sum(importance_factors * band_partition, axis=0)) / weight_total
    variance = lax.optimization_barrier(jnp.sum(importance_factors * (band_partition - sample_average_map) ** 2, axis=0)) / weight_total
    rounded = lax.optimization_barrier(band_partition.astype(jnp.bfloat16)).astype(jnp.float32)
    sources = jnp.transpose(rounded, (2, 0, 1, 3, 4))
    picked = jnp.take_along_axis(sources, offspring.astype(jnp.int32)[:, :, None, None, None], axis=1)
    sample_duplicates = jnp.transpose(picked, (1, 2, 0, 3, 4))
    cell_weight_value = localize.reshape(ZONE_BANDS_NUM, BAND_LATITUDES, LATTICE_WIDTH)[None, None]
    spread_offset = cell_weight_value * (sample_duplicates - sample_average_map) + (1.0 - cell_weight_value) * (band_partition - sample_average_map)
    spread = lax.optimization_barrier(jnp.mean(spread_offset * spread_offset, axis=0))
    scale_ratio = jnp.sqrt((variance + small_eps) / (spread + small_eps))
    posterior = sample_average_map + scale_ratio * spread_offset
    return posterior.reshape(SAMPLE_TOTAL, VERTICAL_QUANTS, NY, LATTICE_WIDTH)
```

```python
import functools

import jax
import jax.numpy as jnp
from jax import lax
from jax.experimental import pallas as pl
from jax.experimental.pallas import tpu as pltpu
from jax.sharding import PartitionSpec as P

MESH = pl.DeviceIdType.MESH
wave_gain = 0.25
advect_gain = 0.1
diffuse_gain = 0.1
small_eps = 1e-05
LANES = 128


def rolled(block, shift):
    flat = block.reshape(-1, block.shape[-1])
    return pltpu.roll(flat, shift % block.shape[-1], 1).reshape(block.shape)


def advance(state):
    fields, rows, members, width = state.shape
    centre = state[:, 1:-1]
    upper = state[:, 2:]
    lower = state[:, :-2]
    right = rolled(centre, -1)
    left = rolled(centre, 1)
    height, east, north = centre[0], centre[1], centre[2]
    new_height = height - (0.5 * wave_gain) * ((right[1] - left[1]) + (upper[2] - lower[2]))
    new_east = east - (0.5 * wave_gain) * (right[0] - left[0])
    new_north = north - (0.5 * wave_gain) * (upper[0] - lower[0])
    gain_e = (0.5 * advect_gain) * east
    gain_n = (0.5 * advect_gain) * north
    t_right, t_left, t_up, t_low, t_mid = right[3:], left[3:], upper[3:], lower[3:], centre[3:]
    laplace = t_right + t_left + t_up + t_low - 4.0 * t_mid
    new_tracer = (
        t_mid
        - (gain_e[None] * (t_right - t_left) + gain_n[None] * (t_up - t_low))
        + diffuse_gain * laplace
    )
    return jnp.concatenate([new_height[None], new_east[None], new_north[None], new_tracer], axis=0)


def kernel(
    n, regs, per, x_ref, w_ref, off_ref, loc_ref, out_ref,
    own, low, high, sendb, recv, postb, locs,
    halo_send, halo_recv, to_send, to_recv, back_send, back_recv,
):
    fields, rows, members, width = x_ref.shape
    halves = width // LANES
    me = lax.axis_index("mem")
    band = lax.axis_index("reg")
    above = lax.rem(band + 1, regs)
    below = lax.rem(band + regs - 1, regs)

    barrier = pltpu.get_barrier_semaphore()
    for o in range(1, n):
        pl.semaphore_signal(barrier, inc=1, device_id={"mem": lax.rem(me + o, n)}, device_id_type=MESH)
    for target in (above, below):
        pl.semaphore_signal(barrier, inc=1, device_id={"reg": target}, device_id_type=MESH)
    own[...] = x_ref[...].astype(own.dtype)
    pl.semaphore_wait(barrier, n + 1)

    halos = []
    for i, (target, dst) in enumerate(((above, low), (below, high))):
        copy = pltpu.make_async_remote_copy(
            src_ref=own, dst_ref=dst, send_sem=halo_send.at[i], recv_sem=halo_recv.at[i],
            device_id={"reg": target}, device_id_type=MESH,
        )
        copy.start()
        halos.append(copy)

    for r in range(rows):
        for c in range(halves):
            locs[r * halves + c] = loc_ref[r:r + 1, c * LANES:(c + 1) * LANES]
    eye = lax.broadcasted_iota(jnp.int32, (members, members), 0) == lax.broadcasted_iota(
        jnp.int32, (members, members), 1
    )
    column = jnp.sum(jnp.where(eye, jnp.broadcast_to(w_ref[...], (members, members)), 0.0), axis=1, keepdims=True)
    wide = jnp.broadcast_to(column, (members, LANES))
    total_slabs = fields * rows * halves
    for d in range(n):
        sendb[d, per] = wide
    for k in range(total_slabs, n * per):
        sendb[k // per, k % per] = jnp.zeros((members, LANES), jnp.float32)
    everyone = n * members
    pick = (
        lax.broadcasted_iota(jnp.int32, (everyone, everyone), 0)
        == jnp.broadcast_to(off_ref[...], (everyone, everyone))
    ).astype(jnp.float32).astype(jnp.bfloat16)

    for copy in halos:
        copy.wait_recv()
    state = jnp.concatenate(
        [low[...].astype(jnp.float32), x_ref[...], high[...].astype(jnp.float32)], axis=1
    )
    state = advance(advance(state))
    for f in range(fields):
        for r in range(rows):
            for c in range(halves):
                k = (f * rows + r) * halves + c
                sendb[k // per, k % per] = state[f, r, :, c * LANES:(c + 1) * LANES]

    outgoing = []
    for o in range(1, n):
        peer = lax.rem(me + o, n)
        copy = pltpu.make_async_remote_copy(
            src_ref=sendb.at[peer], dst_ref=recv.at[:, me],
            send_sem=to_send.at[o - 1], recv_sem=to_recv.at[o - 1],
            device_id={"mem": peer}, device_id_type=MESH,
        )
        copy.start()
        outgoing.append(copy)
    for s in range(per + 1):
        recv[s, me] = sendb[me, s]
    for copy in outgoing:
        copy.wait_recv()

    weight = recv[per].reshape(everyone, LANES)
    total = jnp.sum(weight, axis=0, keepdims=True)
    for s in range(per):
        cast = recv[s].reshape(everyone, LANES)
        mean = jnp.sum(weight * cast, axis=0, keepdims=True) / total
        departure = cast - mean
        variance = jnp.sum(weight * departure * departure, axis=0, keepdims=True) / total
        copies = lax.dot_general(
            pick, cast.astype(jnp.bfloat16), (((0,), (0,)), ((), ())), preferred_element_type=jnp.float32
        )
        local = locs[lax.rem(me * per + s, rows * halves)]
        deviation = local * (copies - mean) + (1.0 - local) * departure
        spread = jnp.sum(deviation * deviation, axis=0, keepdims=True) / everyone
        ratio = jnp.sqrt((variance + small_eps) / (spread + small_eps))
        postb[:, s] = (mean + ratio * deviation).reshape(n, members, LANES)

    returned = []
    for o in range(1, n):
        peer = lax.rem(me + o, n)
        copy = pltpu.make_async_remote_copy(
            src_ref=postb.at[peer], dst_ref=out_ref.at[me],
            send_sem=back_send.at[o - 1], recv_sem=back_recv.at[o - 1],
            device_id={"mem": peer}, device_id_type=MESH,
        )
        copy.start()
        returned.append(copy)
    for s in range(per):
        out_ref[me, s] = postb[me, s]
    for copy in halos + outgoing:
        copy.wait_send()
    for copy in returned:
        copy.wait()


def solution(mesh):
    n, regs = mesh.shape["mem"], mesh.shape["reg"]

    def per_device(sample_stack, weights, offspring, localize):
        members, fields, rows, width = sample_stack.shape
        slabs = fields * rows * (width // LANES)
        per = -(-slabs // n)
        x = jnp.transpose(sample_stack, (1, 2, 0, 3))
        vmem = pl.BlockSpec(memory_space=pltpu.VMEM)
        sem = pltpu.SemaphoreType.DMA
        out = pl.pallas_call(
            functools.partial(kernel, n, regs, per),
            out_shape=jax.ShapeDtypeStruct((n, per, members, LANES), jnp.float32),
            in_specs=[vmem] * 4,
            out_specs=vmem,
            scratch_shapes=[
                pltpu.VMEM(x.shape, jnp.bfloat16),
                pltpu.VMEM(x.shape, jnp.bfloat16),
                pltpu.VMEM(x.shape, jnp.bfloat16),
                pltpu.VMEM((n, per + 1, members, LANES), jnp.float32),
                pltpu.VMEM((per + 1, n, members, LANES), jnp.float32),
                pltpu.VMEM((n, per, members, LANES), jnp.float32),
                pltpu.VMEM((rows * (width // LANES), 1, LANES), jnp.float32),
                sem((2,)), sem((2,)), sem((n - 1,)), sem((n - 1,)), sem((n - 1,)), sem((n - 1,)),
            ],
            compiler_params=pltpu.CompilerParams(
                collective_id=0, has_side_effects=True, vmem_limit_bytes=32 << 20
            ),
        )(x, weights, offspring, localize)
        out = out.reshape(n * per, members, LANES)[:slabs]
        out = out.reshape(fields, rows, width // LANES, members, LANES)
        return jnp.transpose(out, (3, 0, 1, 2, 4)).reshape(members, fields, rows, width)

    in_specs = (P("mem", None, "reg", None), P("reg", "mem"), P("reg", None), P("reg", None))
    return jax.shard_map(
        per_device, mesh=mesh, in_specs=in_specs, out_specs=P("mem", None, "reg", None), check_vma=False
    )
```

```python
import functools

import jax
import jax.numpy as jnp
from jax import lax
from jax.experimental import pallas as pl
from jax.experimental.pallas import tpu as pltpu
from jax.sharding import PartitionSpec as P

MESH = pl.DeviceIdType.MESH
wave_gain = 0.25
advect_gain = 0.1
diffuse_gain = 0.1
small_eps = 1e-05
LANES = 128


def rolled(block, shift):
    flat = block.reshape(-1, block.shape[-1])
    return pltpu.roll(flat, shift % block.shape[-1], 1).reshape(block.shape)


def wave(height, east, north):
    mid = slice(1, -1)
    gain = 0.5 * wave_gain
    inner, flow = height[mid], east[mid]
    new_height = inner - gain * ((rolled(flow, -1) - rolled(flow, 1)) + (north[2:] - north[:-2]))
    new_east = flow - gain * (rolled(inner, -1) - rolled(inner, 1))
    new_north = north[mid] - gain * (height[2:] - height[:-2])
    return new_height, new_east, new_north


def carried(tracer, gain_e, gain_n):
    centre, upper, lower = tracer[:, 1:-1], tracer[:, 2:], tracer[:, :-2]
    right, left = rolled(centre, -1), rolled(centre, 1)
    laplace = right + left + upper + lower - 4.0 * centre
    slopes = gain_e[None] * (right - left) + gain_n[None] * (upper - lower)
    return centre - slopes + diffuse_gain * laplace


def kernel(
    n, regs, per, group, x_ref, w_hbm, off_hbm, loc_hbm, out_ref,
    w_ref, off_ref, loc_ref,
    xin, xown, own, low, high, sendb, recv, postb, locs, wbuf, wrecv,
    in_sem, halo_send, halo_recv, w_send, w_recv, to_send, to_recv, back_send, back_recv,
):
    members, fields, rows, width = x_ref.shape
    halves = width // LANES
    block = rows * halves
    me = lax.axis_index("mem")
    band = lax.axis_index("reg")
    above = lax.rem(band + 1, regs)
    below = lax.rem(band + regs - 1, regs)
    peers = [lax.rem(me + o, n) for o in range(1, n)]
    chunks = []
    for p in range(0, per, group):
        q = min(p + group, per)
        chunks.append((p, q, p * n // block, min(q * n // block, fields)))

    loads = []
    for i, (p, q, f, g) in enumerate(chunks):
        copy = pltpu.make_async_copy(x_ref.at[:, f:g], xin.at[:, f:g], in_sem.at[i])
        copy.start()
        loads.append(copy)
    small = []
    for i, (src, dst) in enumerate(((w_hbm, w_ref), (off_hbm, off_ref), (loc_hbm, loc_ref))):
        copy = pltpu.make_async_copy(src, dst, in_sem.at[len(chunks) + i])
        copy.start()
        small.append(copy)
    barrier = pltpu.get_barrier_semaphore()
    for target in (above, below):
        pl.semaphore_signal(barrier, inc=1, device_id={"reg": target}, device_id_type=MESH)
    for peer in peers:
        pl.semaphore_signal(barrier, inc=1, device_id={"mem": peer}, device_id_type=MESH)

    halos = []
    for i, (p, q, f, g) in enumerate(chunks):
        loads[i].wait()
        for k in range(f, g):
            for r in range(rows):
                piece = xin[:, k, r, :]
                xown[k, r] = piece
                own[k, r] = piece.astype(own.dtype)
        if i == 0:
            pl.semaphore_wait(barrier, n + 1)
        pair = []
        for j, (target, dst) in enumerate(((above, low), (below, high))):
            copy = pltpu.make_async_remote_copy(
                src_ref=own.at[f:g], dst_ref=dst.at[f:g],
                send_sem=halo_send.at[2 * i + j], recv_sem=halo_recv.at[2 * i + j],
                device_id={"reg": target}, device_id_type=MESH,
            )
            copy.start()
            pair.append(copy)
        halos.append(pair)

    for copy in small:
        copy.wait()
    eye = lax.broadcasted_iota(jnp.int32, (members, members), 0) == lax.broadcasted_iota(
        jnp.int32, (members, members), 1
    )
    column = jnp.sum(jnp.where(eye, jnp.broadcast_to(w_ref[...], (members, members)), 0.0), axis=1, keepdims=True)
    wide = jnp.broadcast_to(column, (members, LANES))
    wbuf[...] = wide
    shares = []
    for o, peer in enumerate(peers):
        copy = pltpu.make_async_remote_copy(
            src_ref=wbuf, dst_ref=wrecv.at[me], send_sem=w_send.at[o], recv_sem=w_recv.at[o],
            device_id={"mem": peer}, device_id_type=MESH,
        )
        copy.start()
        shares.append(copy)
    wrecv[me] = wide
    for r in range(rows):
        for c in range(halves):
            locs[r * halves + c] = loc_ref[r:r + 1, c * LANES:(c + 1) * LANES]
    slabs = fields * block
    for k in range(slabs, n * per):
        sendb[k % n, k // n] = jnp.zeros((members, LANES), jnp.float32)
    everyone = n * members
    pick = (
        lax.broadcasted_iota(jnp.int32, (everyone, everyone), 0)
        == jnp.broadcast_to(off_ref[...], (everyone, everyone))
    ).astype(jnp.float32).astype(jnp.bfloat16)

    def store(field, value):
        for r in range(rows):
            for c in range(halves):
                k = (field * rows + r) * halves + c
                sendb[k % n, k // n] = value[r, :, c * LANES:(c + 1) * LANES]

    held = {}

    def forecast(i):
        p, q, f, g = chunks[i]
        for copy in halos[i]:
            copy.wait_recv()
        state = jnp.concatenate(
            [low[f:g].astype(jnp.float32), xown[f:g], high[f:g].astype(jnp.float32)], axis=1
        )
        first = 0
        if i == 0:
            height, east, north = state[0], state[1], state[2]
            held["e0"] = (0.5 * advect_gain) * east[1:-1]
            held["n0"] = (0.5 * advect_gain) * north[1:-1]
            height, east, north = wave(height, east, north)
            held["e1"] = (0.5 * advect_gain) * east[1:-1]
            held["n1"] = (0.5 * advect_gain) * north[1:-1]
            for field, value in enumerate(wave(height, east, north)):
                store(field, value)
            first = 3
        tracer = carried(state[first:], held["e0"], held["n0"])
        tracer = carried(tracer, held["e1"], held["n1"])
        for field in range(f + first, g):
            store(field, tracer[field - f - first])
        copies = []
        for o, peer in enumerate(peers):
            slot = i * (n - 1) + o
            copy = pltpu.make_async_remote_copy(
                src_ref=sendb.at[peer, p:q], dst_ref=recv.at[p:q, me],
                send_sem=to_send.at[slot], recv_sem=to_recv.at[slot],
                device_id={"mem": peer}, device_id_type=MESH,
            )
            copy.start()
            copies.append(copy)
        for s in range(p, q):
            recv[s, me] = sendb[me, s]
        return copies

    def analyse(i, arrivals):
        p, q, f, g = chunks[i]
        for copy in arrivals:
            copy.wait_recv()
        if i == 0:
            for copy in shares:
                copy.wait_recv()
            held["w"] = wrecv[...].reshape(everyone, LANES)
            held["total"] = jnp.sum(held["w"], axis=0, keepdims=True)
        weight, total = held["w"], held["total"]
        for s in range(p, q):
            cast = recv[s].reshape(everyone, LANES)
            mean = jnp.sum(weight * cast, axis=0, keepdims=True) / total
            departure = cast - mean
            variance = jnp.sum(weight * departure * departure, axis=0, keepdims=True) / total
            copies = lax.dot_general(
                pick, cast.astype(jnp.bfloat16), (((0,), (0,)), ((), ())), preferred_element_type=jnp.float32
            )
            local = locs[lax.rem(me + s * n, block)]
            deviation = local * (copies - mean) + (1.0 - local) * departure
            spread = jnp.sum(deviation * deviation, axis=0, keepdims=True) / everyone
            ratio = jnp.sqrt((variance + small_eps) / (spread + small_eps))
            postb[:, s] = (mean + ratio * deviation).reshape(n, members, LANES)
        copies = []
        for o, peer in enumerate(peers):
            slot = i * (n - 1) + o
            copy = pltpu.make_async_remote_copy(
                src_ref=postb.at[peer, p:q], dst_ref=out_ref.at[p:q, me],
                send_sem=back_send.at[slot], recv_sem=back_recv.at[slot],
                device_id={"mem": peer}, device_id_type=MESH,
            )
            copy.start()
            copies.append(copy)
        for s in range(p, q):
            out_ref[s, me] = postb[me, s]
        return copies

    sent, returned = [], []
    last = len(chunks) - 1
    for i in range(last + 1):
        sent.append(forecast(i))
        if i >= 1:
            returned.append(analyse(i - 1, sent[i - 1]))
    returned.append(analyse(last, sent[last]))

    for pair in halos:
        for copy in pair:
            copy.wait_send()
    for copy in shares + sum(sent, []):
        copy.wait_send()
    for copy in sum(returned, []):
        copy.wait()


def solution(mesh):
    n, regs = mesh.shape["mem"], mesh.shape["reg"]

    def per_device(sample_stack, weights, offspring, localize):
        members, fields, rows, width = sample_stack.shape
        halves = width // LANES
        slabs = fields * rows * halves
        per = -(-slabs // n)
        group = max(1, 16 // n)
        steps = -(-per // group)
        turned = (fields, rows, members, width)
        vmem = pl.BlockSpec(memory_space=pltpu.VMEM)
        sem = pltpu.SemaphoreType.DMA
        out = pl.pallas_call(
            functools.partial(kernel, n, regs, per, group),
            out_shape=jax.ShapeDtypeStruct((per, n, members, LANES), jnp.float32),
            in_specs=[pl.BlockSpec(memory_space=pltpu.HBM)] * 4,
            out_specs=vmem,
            scratch_shapes=[
                pltpu.VMEM(weights.shape, weights.dtype),
                pltpu.VMEM(offspring.shape, offspring.dtype),
                pltpu.VMEM(localize.shape, localize.dtype),
                pltpu.VMEM(sample_stack.shape, jnp.float32),
                pltpu.VMEM(turned, jnp.float32),
                pltpu.VMEM(turned, jnp.bfloat16),
                pltpu.VMEM(turned, jnp.bfloat16),
                pltpu.VMEM(turned, jnp.bfloat16),
                pltpu.VMEM((n, per, members, LANES), jnp.float32),
                pltpu.VMEM((per, n, members, LANES), jnp.float32),
                pltpu.VMEM((n, per, members, LANES), jnp.float32),
                pltpu.VMEM((rows * halves, 1, LANES), jnp.float32),
                pltpu.VMEM((members, LANES), jnp.float32),
                pltpu.VMEM((n, members, LANES), jnp.float32),
                sem((steps + 3,)), sem((2 * steps,)), sem((2 * steps,)), sem((n - 1,)), sem((n - 1,)),
                sem((steps * (n - 1),)), sem((steps * (n - 1),)), sem((steps * (n - 1),)), sem((steps * (n - 1),)),
            ],
            compiler_params=pltpu.CompilerParams(
                collective_id=0, has_side_effects=True, vmem_limit_bytes=32 << 20
            ),
        )(sample_stack, weights, offspring, localize)
        out = out.reshape(n * per, members, LANES)[:slabs]
        out = out.reshape(fields, rows, halves, members, LANES)
        return jnp.transpose(out, (3, 0, 1, 2, 4)).reshape(members, fields, rows, width)

    in_specs = (P("mem", None, "reg", None), P("reg", "mem"), P("reg", None), P("reg", None))
    return jax.shard_map(
        per_device, mesh=mesh, in_specs=in_specs, out_specs=P("mem", None, "reg", None), check_vma=False
    )
```

```python
import functools

import jax
import jax.numpy as jnp
from jax import lax
from jax.experimental import pallas as pl
from jax.experimental.pallas import tpu as pltpu
from jax.sharding import PartitionSpec as P

MESH = pl.DeviceIdType.MESH
wave_gain = 0.25
advect_gain = 0.1
diffuse_gain = 0.1
small_eps = 1e-05
LANES = 128


def rolled(block, shift):
    flat = block.reshape(-1, block.shape[-1])
    return pltpu.roll(flat, shift % block.shape[-1], 1).reshape(block.shape)


def wave(height, east, north):
    mid = slice(1, -1)
    gain = 0.5 * wave_gain
    inner, flow = height[mid], east[mid]
    new_height = inner - gain * ((rolled(flow, -1) - rolled(flow, 1)) + (north[2:] - north[:-2]))
    new_east = flow - gain * (rolled(inner, -1) - rolled(inner, 1))
    new_north = north[mid] - gain * (height[2:] - height[:-2])
    return new_height, new_east, new_north


def carried(tracer, gain_e, gain_n):
    centre, upper, lower = tracer[:, 1:-1], tracer[:, 2:], tracer[:, :-2]
    right, left = rolled(centre, -1), rolled(centre, 1)
    laplace = right + left + upper + lower - 4.0 * centre
    slopes = gain_e[None] * (right - left) + gain_n[None] * (upper - lower)
    return centre - slopes + diffuse_gain * laplace


def kernel(
    n, regs, per, group, x_ref, w_hbm, off_hbm, loc_hbm, out_ref,
    w_ref, off_ref, loc_ref,
    xin, xown, own, low, high, sendb, recv, postb, locs, wbuf, wrecv, back,
    in_sem, halo_send, halo_recv, w_send, w_recv, to_send, to_recv, back_send, back_recv,
):
    members, fields, rows, width = x_ref.shape
    halves = width // LANES
    block = rows * halves
    me = lax.axis_index("mem")
    band = lax.axis_index("reg")
    above = lax.rem(band + 1, regs)
    below = lax.rem(band + regs - 1, regs)
    peers = [lax.rem(me + o, n) for o in range(1, n)]
    chunks = []
    for p in range(0, per, group):
        q = min(p + group, per)
        chunks.append((p, q, p * n // block, min(q * n // block, fields)))

    loads = []
    for i, (p, q, f, g) in enumerate(chunks):
        copy = pltpu.make_async_copy(x_ref.at[:, f:g], xin.at[:, f:g], in_sem.at[i])
        copy.start()
        loads.append(copy)
    small = []
    for i, (src, dst) in enumerate(((w_hbm, w_ref), (off_hbm, off_ref), (loc_hbm, loc_ref))):
        copy = pltpu.make_async_copy(src, dst, in_sem.at[len(chunks) + i])
        copy.start()
        small.append(copy)
    barrier = pltpu.get_barrier_semaphore()
    for target in (above, below):
        pl.semaphore_signal(barrier, inc=1, device_id={"reg": target}, device_id_type=MESH)
    for peer in peers:
        pl.semaphore_signal(barrier, inc=1, device_id={"mem": peer}, device_id_type=MESH)

    halos = []
    for i, (p, q, f, g) in enumerate(chunks):
        loads[i].wait()
        for k in range(f, g):
            for r in range(rows):
                piece = xin[:, k, r, :]
                xown[k, r] = piece
                own[k, r] = piece.astype(own.dtype)
        if i == 0:
            pl.semaphore_wait(barrier, n + 1)
        pair = []
        for j, (target, dst) in enumerate(((above, low), (below, high))):
            copy = pltpu.make_async_remote_copy(
                src_ref=own.at[f:g], dst_ref=dst.at[f:g],
                send_sem=halo_send.at[2 * i + j], recv_sem=halo_recv.at[2 * i + j],
                device_id={"reg": target}, device_id_type=MESH,
            )
            copy.start()
            pair.append(copy)
        halos.append(pair)

    for copy in small:
        copy.wait()
    eye = lax.broadcasted_iota(jnp.int32, (members, members), 0) == lax.broadcasted_iota(
        jnp.int32, (members, members), 1
    )
    column = jnp.sum(jnp.where(eye, jnp.broadcast_to(w_ref[...], (members, members)), 0.0), axis=1, keepdims=True)
    wide = jnp.broadcast_to(column, (members, LANES))
    wbuf[...] = wide
    shares = []
    for o, peer in enumerate(peers):
        copy = pltpu.make_async_remote_copy(
            src_ref=wbuf, dst_ref=wrecv.at[me], send_sem=w_send.at[o], recv_sem=w_recv.at[o],
            device_id={"mem": peer}, device_id_type=MESH,
        )
        copy.start()
        shares.append(copy)
    wrecv[me] = wide
    for r in range(rows):
        for c in range(halves):
            locs[r * halves + c] = loc_ref[r:r + 1, c * LANES:(c + 1) * LANES]
    slabs = fields * block
    for k in range(slabs, n * per):
        sendb[k % n, k // n] = jnp.zeros((members, LANES), jnp.float32)
    everyone = n * members
    pick = (
        lax.broadcasted_iota(jnp.int32, (everyone, everyone), 0)
        == jnp.broadcast_to(off_ref[...], (everyone, everyone))
    ).astype(jnp.float32).astype(jnp.bfloat16)

    def store(field, value):
        for r in range(rows):
            for c in range(halves):
                k = (field * rows + r) * halves + c
                sendb[k % n, k // n] = value[r, :, c * LANES:(c + 1) * LANES]

    held = {}

    def forecast(i):
        p, q, f, g = chunks[i]
        for copy in halos[i]:
            copy.wait_recv()
        state = jnp.concatenate(
            [low[f:g].astype(jnp.float32), xown[f:g], high[f:g].astype(jnp.float32)], axis=1
        )
        first = 0
        if i == 0:
            height, east, north = state[0], state[1], state[2]
            held["e0"] = (0.5 * advect_gain) * east[1:-1]
            held["n0"] = (0.5 * advect_gain) * north[1:-1]
            height, east, north = wave(height, east, north)
            held["e1"] = (0.5 * advect_gain) * east[1:-1]
            held["n1"] = (0.5 * advect_gain) * north[1:-1]
            for field, value in enumerate(wave(height, east, north)):
                store(field, value)
            first = 3
        tracer = carried(state[first:], held["e0"], held["n0"])
        tracer = carried(tracer, held["e1"], held["n1"])
        for field in range(f + first, g):
            store(field, tracer[field - f - first])
        copies = []
        for o, peer in enumerate(peers):
            slot = i * (n - 1) + o
            copy = pltpu.make_async_remote_copy(
                src_ref=sendb.at[peer, p:q], dst_ref=recv.at[p:q, me],
                send_sem=to_send.at[slot], recv_sem=to_recv.at[slot],
                device_id={"mem": peer}, device_id_type=MESH,
            )
            copy.start()
            copies.append(copy)
        for s in range(p, q):
            recv[s, me] = sendb[me, s]
        return copies

    def analyse(i, arrivals):
        p, q, f, g = chunks[i]
        for copy in arrivals:
            copy.wait_recv()
        if i == 0:
            for copy in shares:
                copy.wait_recv()
            held["w"] = wrecv[...].reshape(everyone, LANES)
            held["total"] = jnp.sum(held["w"], axis=0, keepdims=True)
        weight, total = held["w"], held["total"]
        for s in range(p, q):
            cast = recv[s].reshape(everyone, LANES)
            mean = jnp.sum(weight * cast, axis=0, keepdims=True) / total
            departure = cast - mean
            variance = jnp.sum(weight * departure * departure, axis=0, keepdims=True) / total
            copies = lax.dot_general(
                pick, cast.astype(jnp.bfloat16), (((0,), (0,)), ((), ())), preferred_element_type=jnp.float32
            )
            local = locs[lax.rem(me + s * n, block)]
            deviation = local * (copies - mean) + (1.0 - local) * departure
            spread = jnp.sum(deviation * deviation, axis=0, keepdims=True) / everyone
            ratio = jnp.sqrt((variance + small_eps) / (spread + small_eps))
            postb[:, s] = (mean + ratio * deviation).reshape(n, members, LANES)
        copies = []
        for o, peer in enumerate(peers):
            slot = i * (n - 1) + o
            copy = pltpu.make_async_remote_copy(
                src_ref=postb.at[peer, p:q], dst_ref=back.at[p:q, me],
                send_sem=back_send.at[slot], recv_sem=back_recv.at[slot],
                device_id={"mem": peer}, device_id_type=MESH,
            )
            copy.start()
            copies.append(copy)
        for s in range(p, q):
            back[s, me] = postb[me, s]
        return copies

    sent, returned = [], []
    last = len(chunks) - 1
    for i in range(last + 1):
        sent.append(forecast(i))
        if i >= 1:
            returned.append(analyse(i - 1, sent[i - 1]))
    returned.append(analyse(last, sent[last]))

    for pair in halos:
        for copy in pair:
            copy.wait_send()
    for copy in shares + sum(sent, []):
        copy.wait_send()
    for copy in sum(returned, []):
        copy.wait()
    for field in range(fields):
        for r in range(rows):
            for c in range(halves):
                k = (field * rows + r) * halves + c
                out_ref[:, field, r, c * LANES:(c + 1) * LANES] = back[k // n, k % n]


def solution(mesh):
    n, regs = mesh.shape["mem"], mesh.shape["reg"]

    def per_device(sample_stack, weights, offspring, localize):
        members, fields, rows, width = sample_stack.shape
        halves = width // LANES
        slabs = fields * rows * halves
        per = -(-slabs // n)
        group = max(1, 48 // n)
        steps = -(-per // group)
        turned = (fields, rows, members, width)
        vmem = pl.BlockSpec(memory_space=pltpu.VMEM)
        sem = pltpu.SemaphoreType.DMA
        out = pl.pallas_call(
            functools.partial(kernel, n, regs, per, group),
            out_shape=jax.ShapeDtypeStruct(sample_stack.shape, jnp.float32),
            in_specs=[pl.BlockSpec(memory_space=pltpu.HBM)] * 4,
            out_specs=vmem,
            scratch_shapes=[
                pltpu.VMEM(weights.shape, weights.dtype),
                pltpu.VMEM(offspring.shape, offspring.dtype),
                pltpu.VMEM(localize.shape, localize.dtype),
                pltpu.VMEM(sample_stack.shape, jnp.float32),
                pltpu.VMEM(turned, jnp.float32),
                pltpu.VMEM(turned, jnp.bfloat16),
                pltpu.VMEM(turned, jnp.bfloat16),
                pltpu.VMEM(turned, jnp.bfloat16),
                pltpu.VMEM((n, per, members, LANES), jnp.float32),
                pltpu.VMEM((per, n, members, LANES), jnp.float32),
                pltpu.VMEM((n, per, members, LANES), jnp.float32),
                pltpu.VMEM((rows * halves, 1, LANES), jnp.float32),
                pltpu.VMEM((members, LANES), jnp.float32),
                pltpu.VMEM((n, members, LANES), jnp.float32),
                pltpu.VMEM((per, n, members, LANES), jnp.float32),
                sem((steps + 3,)), sem((2 * steps,)), sem((2 * steps,)), sem((n - 1,)), sem((n - 1,)),
                sem((steps * (n - 1),)), sem((steps * (n - 1),)), sem((steps * (n - 1),)), sem((steps * (n - 1),)),
            ],
            compiler_params=pltpu.CompilerParams(
                collective_id=0, has_side_effects=True, vmem_limit_bytes=60 << 20
            ),
        )(sample_stack, weights, offspring, localize)
        return out

    in_specs = (P("mem", None, "reg", None), P("reg", "mem"), P("reg", None), P("reg", None))
    return jax.shard_map(
        per_device, mesh=mesh, in_specs=in_specs, out_specs=P("mem", None, "reg", None), check_vma=False
    )
```

```python
import functools

import jax
import jax.numpy as jnp
from jax import lax
from jax.experimental import pallas as pl
from jax.experimental.pallas import tpu as pltpu
from jax.sharding import PartitionSpec as P

MESH = pl.DeviceIdType.MESH
wave_gain = 0.25
advect_gain = 0.1
diffuse_gain = 0.1
small_eps = 1e-05
LANES = 128


def rolled(block, shift):
    flat = block.reshape(-1, block.shape[-1])
    return pltpu.roll(flat, shift % block.shape[-1], 1).reshape(block.shape)


def wave(height, east, north):
    mid = slice(1, -1)
    gain = 0.5 * wave_gain
    inner, flow = height[mid], east[mid]
    new_height = inner - gain * ((rolled(flow, -1) - rolled(flow, 1)) + (north[2:] - north[:-2]))
    new_east = flow - gain * (rolled(inner, -1) - rolled(inner, 1))
    new_north = north[mid] - gain * (height[2:] - height[:-2])
    return new_height, new_east, new_north


def carried(tracer, gain_e, gain_n):
    centre, upper, lower = tracer[:, 1:-1], tracer[:, 2:], tracer[:, :-2]
    right, left = rolled(centre, -1), rolled(centre, 1)
    laplace = right + left + upper + lower - 4.0 * centre
    slopes = gain_e[None] * (right - left) + gain_n[None] * (upper - lower)
    return centre - slopes + diffuse_gain * laplace


def kernel(
    n, regs, per, group, x_ref, w_hbm, off_hbm, loc_hbm, out_ref,
    w_ref, off_ref, loc_ref,
    xin, xown, own, low, high, sendb, recv, postb, locs, wbuf, wrecv, back,
    in_sem, halo_send, halo_recv, w_send, w_recv, to_send, to_recv, back_send, back_recv,
):
    fields, rows, members, width = x_ref.shape
    halves = width // LANES
    block = rows * halves
    me = lax.axis_index("mem")
    band = lax.axis_index("reg")
    above = lax.rem(band + 1, regs)
    below = lax.rem(band + regs - 1, regs)
    peers = [lax.rem(me + o, n) for o in range(1, n)]
    chunks = []
    for p in range(0, per, group):
        q = min(p + group, per)
        chunks.append((p, q, p * n // block, min(q * n // block, fields)))

    xown = x_ref
    small = []
    for i, (src, dst) in enumerate(((w_hbm, w_ref), (off_hbm, off_ref), (loc_hbm, loc_ref))):
        copy = pltpu.make_async_copy(src, dst, in_sem.at[len(chunks) + i])
        copy.start()
        small.append(copy)
    barrier = pltpu.get_barrier_semaphore()
    for target in (above, below):
        pl.semaphore_signal(barrier, inc=1, device_id={"reg": target}, device_id_type=MESH)
    for peer in peers:
        pl.semaphore_signal(barrier, inc=1, device_id={"mem": peer}, device_id_type=MESH)

    halos = []
    for i, (p, q, f, g) in enumerate(chunks):
        own[f:g] = x_ref[f:g].astype(own.dtype)
        if i == 0:
            pl.semaphore_wait(barrier, n + 1)
        pair = []
        for j, (target, dst) in enumerate(((above, low), (below, high))):
            copy = pltpu.make_async_remote_copy(
                src_ref=own.at[f:g], dst_ref=dst.at[f:g],
                send_sem=halo_send.at[2 * i + j], recv_sem=halo_recv.at[2 * i + j],
                device_id={"reg": target}, device_id_type=MESH,
            )
            copy.start()
            pair.append(copy)
        halos.append(pair)

    for copy in small:
        copy.wait()
    eye = lax.broadcasted_iota(jnp.int32, (members, members), 0) == lax.broadcasted_iota(
        jnp.int32, (members, members), 1
    )
    column = jnp.sum(jnp.where(eye, jnp.broadcast_to(w_ref[...], (members, members)), 0.0), axis=1, keepdims=True)
    wide = jnp.broadcast_to(column, (members, LANES))
    wbuf[...] = wide
    shares = []
    for o, peer in enumerate(peers):
        copy = pltpu.make_async_remote_copy(
            src_ref=wbuf, dst_ref=wrecv.at[me], send_sem=w_send.at[o], recv_sem=w_recv.at[o],
            device_id={"mem": peer}, device_id_type=MESH,
        )
        copy.start()
        shares.append(copy)
    wrecv[me] = wide
    for r in range(rows):
        for c in range(halves):
            locs[r * halves + c] = loc_ref[r:r + 1, c * LANES:(c + 1) * LANES]
    slabs = fields * block
    for k in range(slabs, n * per):
        sendb[k % n, k // n] = jnp.zeros((members, LANES), jnp.float32)
    everyone = n * members
    pick = (
        lax.broadcasted_iota(jnp.int32, (everyone, everyone), 0)
        == jnp.broadcast_to(off_ref[...], (everyone, everyone))
    ).astype(jnp.float32).astype(jnp.bfloat16)

    def store(field, value):
        for r in range(rows):
            for c in range(halves):
                k = (field * rows + r) * halves + c
                sendb[k % n, k // n] = value[r, :, c * LANES:(c + 1) * LANES]

    held = {}

    def forecast(i):
        p, q, f, g = chunks[i]
        for copy in halos[i]:
            copy.wait_recv()
        state = jnp.concatenate(
            [low[f:g].astype(jnp.float32), xown[f:g], high[f:g].astype(jnp.float32)], axis=1
        )
        first = 0
        if i == 0:
            height, east, north = state[0], state[1], state[2]
            held["e0"] = (0.5 * advect_gain) * east[1:-1]
            held["n0"] = (0.5 * advect_gain) * north[1:-1]
            height, east, north = wave(height, east, north)
            held["e1"] = (0.5 * advect_gain) * east[1:-1]
            held["n1"] = (0.5 * advect_gain) * north[1:-1]
            for field, value in enumerate(wave(height, east, north)):
                store(field, value)
            first = 3
        tracer = carried(state[first:], held["e0"], held["n0"])
        tracer = carried(tracer, held["e1"], held["n1"])
        for field in range(f + first, g):
            store(field, tracer[field - f - first])
        copies = []
        for o, peer in enumerate(peers):
            slot = i * (n - 1) + o
            copy = pltpu.make_async_remote_copy(
                src_ref=sendb.at[peer, p:q], dst_ref=recv.at[p:q, me],
                send_sem=to_send.at[slot], recv_sem=to_recv.at[slot],
                device_id={"mem": peer}, device_id_type=MESH,
            )
            copy.start()
            copies.append(copy)
        for s in range(p, q):
            recv[s, me] = sendb[me, s]
        return copies

    def analyse(i, arrivals):
        p, q, f, g = chunks[i]
        for copy in arrivals:
            copy.wait_recv()
        if i == 0:
            for copy in shares:
                copy.wait_recv()
            held["w"] = wrecv[...].reshape(everyone, LANES)
            held["total"] = jnp.sum(held["w"], axis=0, keepdims=True)
        weight, total = held["w"], held["total"]
        for s in range(p, q):
            cast = recv[s].reshape(everyone, LANES)
            mean = jnp.sum(weight * cast, axis=0, keepdims=True) / total
            departure = cast - mean
            variance = jnp.sum(weight * departure * departure, axis=0, keepdims=True) / total
            copies = lax.dot_general(
                pick, cast.astype(jnp.bfloat16), (((0,), (0,)), ((), ())), preferred_element_type=jnp.float32
            )
            local = locs[lax.rem(me + s * n, block)]
            deviation = local * (copies - mean) + (1.0 - local) * departure
            spread = jnp.sum(deviation * deviation, axis=0, keepdims=True) / everyone
            ratio = jnp.sqrt((variance + small_eps) / (spread + small_eps))
            postb[:, s] = (mean + ratio * deviation).reshape(n, members, LANES)
        copies = []
        for o, peer in enumerate(peers):
            slot = i * (n - 1) + o
            copy = pltpu.make_async_remote_copy(
                src_ref=postb.at[peer, p:q], dst_ref=back.at[p:q, me],
                send_sem=back_send.at[slot], recv_sem=back_recv.at[slot],
                device_id={"mem": peer}, device_id_type=MESH,
            )
            copy.start()
            copies.append(copy)
        for s in range(p, q):
            back[s, me] = postb[me, s]
        return copies

    sent, returned = [], []
    last = len(chunks) - 1
    for i in range(last + 1):
        sent.append(forecast(i))
        if i >= 1:
            returned.append(analyse(i - 1, sent[i - 1]))
    returned.append(analyse(last, sent[last]))

    for pair in halos:
        for copy in pair:
            copy.wait_send()
    for copy in shares + sum(sent, []):
        copy.wait_send()
    for copy in sum(returned, []):
        copy.wait()
    for field in range(fields):
        for r in range(rows):
            for c in range(halves):
                k = (field * rows + r) * halves + c
                out_ref[:, field, r, c * LANES:(c + 1) * LANES] = back[k // n, k % n]


def solution(mesh):
    n, regs = mesh.shape["mem"], mesh.shape["reg"]

    def per_device(sample_stack, weights, offspring, localize):
        members, fields, rows, width = sample_stack.shape
        halves = width // LANES
        slabs = fields * rows * halves
        per = -(-slabs // n)
        group = max(1, 48 // n)
        steps = -(-per // group)
        turned = (fields, rows, members, width)
        vmem = pl.BlockSpec(memory_space=pltpu.VMEM)
        sem = pltpu.SemaphoreType.DMA
        out = pl.pallas_call(
            functools.partial(kernel, n, regs, per, group),
            out_shape=jax.ShapeDtypeStruct(sample_stack.shape, jnp.float32),
            in_specs=[vmem] + [pl.BlockSpec(memory_space=pltpu.HBM)] * 3,
            out_specs=vmem,
            scratch_shapes=[
                pltpu.VMEM(weights.shape, weights.dtype),
                pltpu.VMEM(offspring.shape, offspring.dtype),
                pltpu.VMEM(localize.shape, localize.dtype),
                pltpu.VMEM(sample_stack.shape, jnp.float32),
                pltpu.VMEM(turned, jnp.float32),
                pltpu.VMEM(turned, jnp.bfloat16),
                pltpu.VMEM(turned, jnp.bfloat16),
                pltpu.VMEM(turned, jnp.bfloat16),
                pltpu.VMEM((n, per, members, LANES), jnp.float32),
                pltpu.VMEM((per, n, members, LANES), jnp.float32),
                pltpu.VMEM((n, per, members, LANES), jnp.float32),
                pltpu.VMEM((rows * halves, 1, LANES), jnp.float32),
                pltpu.VMEM((members, LANES), jnp.float32),
                pltpu.VMEM((n, members, LANES), jnp.float32),
                pltpu.VMEM((per, n, members, LANES), jnp.float32),
                sem((steps + 3,)), sem((2 * steps,)), sem((2 * steps,)), sem((n - 1,)), sem((n - 1,)),
                sem((steps * (n - 1),)), sem((steps * (n - 1),)), sem((steps * (n - 1),)), sem((steps * (n - 1),)),
            ],
            compiler_params=pltpu.CompilerParams(
                collective_id=0, has_side_effects=True, vmem_limit_bytes=32 << 20
            ),
        )(jnp.transpose(sample_stack, (1, 2, 0, 3)), weights, offspring, localize)
        return out

    in_specs = (P("mem", None, "reg", None), P("reg", "mem"), P("reg", None), P("reg", None))
    return jax.shard_map(
        per_device, mesh=mesh, in_specs=in_specs, out_specs=P("mem", None, "reg", None), check_vma=False
    )
```
